32 devices in a mesh: dp: 8 (over z, x), ctx: 2 (over y), mp: 2 (over core).
Axes of the slice: x: 2, y: 2, z: 4, core: 2. Of those that a mesh axis runs over, the one named last changes fastest.
Arguments:
- frames_in: bfloat16 [12288, 768], P(('dp', 'ctx')), may hold values from -6 to 6
- qkv_weight: bfloat16 [2, 768, 3, 768], P(None, ('dp', 'ctx'), None, 'mp'), may hold values from -0.21875 to 0.21875
- out_weight: bfloat16 [2, 768, 768], P(None, ('dp', 'ctx'), 'mp'), may hold values from -0.4375 to 0.4375
- up_weight: bfloat16 [2, 768, 4, 768], P(None, ('dp', 'ctx'), None, 'mp'), may hold values from -0.21875 to 0.21875
- down_weight: bfloat16 [2, 768, 4, 768], P(None, ('dp', 'ctx'), None, 'mp'), may hold values from -0.109375 to 0.109375
- col_biases: bfloat16 [2, 6, 12, 64], P(None, None, 'mp', ('dp', 'ctx')), may hold values from -3 to 3
- norm_gains: bfloat16 [2, 2, 768], P(None, None, ('dp', 'ctx')), may hold values from 0.5 to 1.5
- row_shifts: bfloat16 [2, 4, 768], P(None, None, ('dp', 'ctx')), may hold values from -3 to 3
- cotangent: bfloat16 [12288, 768], P(('dp', 'ctx')), may hold values from -6 to 6
Outputs:
- frames_out: bfloat16 [12288, 768], P(('dp', 'ctx'))
- frames_grad: float32 [12288, 768], P(('dp', 'ctx'))
- qkv_grad: float32 [2, 768, 3, 768], P(None, ('dp', 'ctx'), None, 'mp')
- out_grad: float32 [2, 768, 768], P(None, ('dp', 'ctx'), 'mp')
- up_grad: float32 [2, 768, 4, 768], P(None, ('dp', 'ctx'), None, 'mp')
- down_grad: float32 [2, 768, 4, 768], P(None, ('dp', 'ctx'), None, 'mp')
- bias_grad: float32 [2, 6, 12, 64], P(None, None, 'mp', ('dp', 'ctx'))
- gain_grad: float32 [2, 2, 768], P(None, None, ('dp', 'ctx'))
- shift_grad: float32 [2, 4, 768], P(None, None, ('dp', 'ctx'))
The draws below stay inside these ranges and needn't reach their ends.
All inputs are finite; a program needn't handle non-finite values.
Results may differ from the reference program's by a relative error of at most 0.0085.
Values may be sent and summed in bfloat16 or wider, within the bound.
No kernel may reach another device: no remote copies, remote signals or barrier semaphores. Data moves between devices by JAX's collectives and lax.ppermute only.
A program may use at most 192 MiB of HBM per device.

```python
import jax
import jax.numpy as jnp
from jax import lax

D = 768
HEADS = 12
HEAD_DIM = 64
FF = 3072
LAYERS = 2
FRAMES = 1536
CLIPS = 8
TOKENS = 12288


def level_of(stream_key, extent, cuts, low, high):
    loudness, own = 1.0, jax.random.fold_in(stream_key, 6)
    for position, shards_of in cuts:
        steps = jnp.exp(jax.random.uniform(jax.random.fold_in(own, position), (shards_of,), jnp.float32, low / len(cuts), high / len(cuts)))
        loudness = loudness * jnp.repeat(steps, extent[position] // shards_of).reshape([-1 if axis == position else 1 for axis in range(len(extent))])
    return loudness


def noise(own_key, extent, scale, reach, cuts=(), kind=jnp.bfloat16):
    loudness = level_of(own_key, extent, cuts, -0.22, 0.18) if cuts else 1.0
    drawn = jax.random.normal(own_key, extent, jnp.float32) * scale * loudness
    return jnp.minimum(jnp.maximum(drawn, -reach), reach).astype(kind)


def setup_inputs(seed: int = 0) -> dict:
    arg_keys = jax.random.split(jax.random.key(seed), 10)
    return {
        "frames_in": noise(arg_keys[0], (TOKENS, D), 1.0, 6.0, ((0, 16),)),
        "qkv_weight": noise(arg_keys[1], (LAYERS, D, 3, D), D ** -0.5, 0.21875, ((1, 16), (3, 2))),
        "out_weight": noise(arg_keys[2], (LAYERS, D, D), (D // 4) ** -0.5, 0.4375, ((1, 16), (2, 2))),
        "up_weight": noise(arg_keys[3], (LAYERS, D, 4, D), D ** -0.5, 0.21875, ((1, 16), (3, 2))),
        "down_weight": noise(arg_keys[4], (LAYERS, D, 4, D), FF ** -0.5, 0.109375, ((1, 16), (3, 2))),
        "col_biases": noise(arg_keys[5], (LAYERS, 6, HEADS, HEAD_DIM), 0.5, 3.0, ((2, 2), (3, 16))),
        "norm_gains": jnp.clip(1.0 + 0.1 * jax.random.normal(arg_keys[6], (LAYERS, 2, D), jnp.float32), 0.5, 1.5).astype(jnp.bfloat16),
        "row_shifts": noise(arg_keys[7], (LAYERS, 4, D), 0.5, 3.0, ((2, 16),)),
        "cotangent": noise(arg_keys[8], (TOKENS, D), 1.0, 6.0, ((0, 16),)),
    }


@jax.custom_vjp
def low(v):
    return lax.optimization_barrier(v.astype(jnp.bfloat16)).astype(jnp.float32)

@jax.custom_vjp
def low_back(v):
    return v

def low_keep(v):
    return (low(v), None)

def low_pass(kept, grad):
    return (grad,)

def back_keep(v):
    return (v, None)

def back_low(kept, grad):
    return (low(grad),)
low.defvjp(low_keep, low_pass)
low_back.defvjp(back_keep, back_low)
exact_mode = lax.Precision.HIGHEST

def both_ways(values_in):
    return low(low_back(values_in))

def layer_norm(values_in, gain, shift):
    middle = lax.optimization_barrier(jnp.mean(values_in, axis=-1, keepdims=True))
    centred = values_in - middle
    spread = lax.optimization_barrier(jnp.mean(centred * centred, axis=-1, keepdims=True))
    return centred * lax.rsqrt(spread + 1e-05) * gain + shift

def clip_attention(pieces):
    queries, keys_in, values_in = pieces
    head_shape = (FRAMES, HEADS, HEAD_DIM)
    scores = jnp.einsum('qhe,khe->hqk', queries.reshape(head_shape), keys_in.reshape(head_shape), precision=exact_mode) * HEAD_DIM ** (-0.5)
    scores = low_back(scores)
    weights = jax.nn.softmax(scores, axis=-1)
    mixture = jnp.einsum('hqk,khe->qhe', low(weights), values_in.reshape(head_shape), precision=exact_mode)
    return mixture.reshape(FRAMES, D)

def forward(frames, qkv_weight, out_weight, up_weight, down_weight, col_biases, norm_gains, row_shifts):
    state = frames
    clip_shape = (CLIPS, FRAMES, D)
    for which_layer in range(LAYERS):
        biases = col_biases[which_layer].reshape(6, D)
        normed = low(layer_norm(state, norm_gains[which_layer, 0], row_shifts[which_layer, 0]))
        project = jnp.einsum('td,dkc->tkc', normed, qkv_weight[which_layer], precision=exact_mode)
        queries = both_ways(project[:, 0] + biases[0])
        keys_all = both_ways(project[:, 1])
        values_all = both_ways(project[:, 2] + biases[1])
        attended = lax.map(jax.checkpoint(clip_attention), (queries.reshape(clip_shape), keys_all.reshape(clip_shape), values_all.reshape(clip_shape)))
        attended = both_ways(attended.reshape(TOKENS, D))
        branch = low_back(jnp.einsum('tk,dk->td', attended, out_weight[which_layer], precision=exact_mode) + row_shifts[which_layer, 1])
        state = state + branch
        normed = low(layer_norm(state, norm_gains[which_layer, 1], row_shifts[which_layer, 2]))
        hidden_pre = low_back(jnp.einsum('td,daj->taj', normed, up_weight[which_layer], precision=exact_mode) + biases[2:6])
        hidden_act = low(jax.nn.gelu(hidden_pre, approximate=False))
        branch = low_back(jnp.einsum('taj,daj->td', hidden_act, down_weight[which_layer], precision=exact_mode) + row_shifts[which_layer, 3])
        state = state + branch
    return state

def reference(frames_in, qkv_weight, out_weight, up_weight, down_weight, col_biases, norm_gains, row_shifts, cotangent):
    inputs = (frames_in.astype(jnp.float32), qkv_weight.astype(jnp.float32), out_weight.astype(jnp.float32), up_weight.astype(jnp.float32), down_weight.astype(jnp.float32), col_biases.astype(jnp.float32), norm_gains.astype(jnp.float32), row_shifts.astype(jnp.float32))
    result, pullback = jax.vjp(forward, *inputs)
    grads = pullback(cotangent.astype(jnp.float32))
    return (result.astype(jnp.bfloat16), grads[0], grads[1], grads[2], grads[3], grads[4], grads[5], grads[6], grads[7])
```

```python
import jax
import jax.numpy as jnp
from jax import lax
from jax.sharding import PartitionSpec as P

HEAD_DIM = 64


root_half = 0.7071067811865476
inv_root_tau = 0.3989422804014327


def norm_forward(values_in, gain, shift):
    middle = jnp.mean(values_in, axis=-1, keepdims=True)
    centred = values_in - middle
    inverse = lax.rsqrt(jnp.mean(centred * centred, axis=-1, keepdims=True) + 1e-05)
    scaled = centred * inverse
    return (scaled * gain + shift, scaled, inverse)


def norm_backward(grad_out, scaled, inverse, gain):
    gain_part = jnp.sum(grad_out * scaled, axis=0)
    shift_part = jnp.sum(grad_out, axis=0)
    weighted = grad_out * gain
    grad_in = inverse * (
        weighted
        - jnp.mean(weighted, axis=-1, keepdims=True)
        - scaled * jnp.mean(weighted * scaled, axis=-1, keepdims=True)
    )
    return (grad_in, gain_part, shift_part)


def gelu_value(pre_act):
    return 0.5 * pre_act * (1.0 + lax.erf(pre_act * root_half))


def gelu_slope(pre_act):
    return (
        0.5 * (1.0 + lax.erf(pre_act * root_half))
        + pre_act * jnp.exp(-0.5 * pre_act * pre_act) * inv_root_tau
    )


def split_heads(matrix):
    return matrix.reshape(matrix.shape[0], -1, HEAD_DIM).transpose(1, 0, 2)


def merge_heads(stacked):
    return stacked.transpose(1, 0, 2).reshape(stacked.shape[1], -1)


def attend(queries, keys_all, values_all):
    scaling = HEAD_DIM ** (-0.5)

    def one_head(head_item):
        query_h, key_h, value_h = head_item
        scores = (
            jnp.einsum("qe,ke->qk", query_h, key_h, preferred_element_type=jnp.float32) * scaling
        )
        row_max = jnp.max(scores, axis=-1, keepdims=True)
        shifted = jnp.exp(scores - row_max)
        row_sum = jnp.sum(shifted, axis=-1, keepdims=True)
        probs = (shifted / row_sum).astype(jnp.bfloat16)
        mixture = jnp.dot(probs, value_h, preferred_element_type=jnp.float32)
        return (mixture, (row_max + jnp.log(row_sum))[:, 0])

    mixtures, log_sums = lax.map(
        one_head, (split_heads(queries), split_heads(keys_all), split_heads(values_all))
    )
    return (merge_heads(mixtures), log_sums)


def attend_back(queries, keys_all, values_all, grad_att, log_sums):
    scaling = HEAD_DIM ** (-0.5)

    def one_head(head_item):
        query_h, key_h, value_h, grad_h, sums_h = head_item
        scores = (
            jnp.einsum("qe,ke->qk", query_h, key_h, preferred_element_type=jnp.float32) * scaling
        )
        probs = jnp.exp(scores - sums_h[:, None])
        grad_p = jnp.einsum("qe,ke->qk", grad_h, value_h, preferred_element_type=jnp.float32)
        inner = jnp.sum(probs * grad_p, axis=-1, keepdims=True)
        grad_s = (probs * (grad_p - inner)).astype(jnp.bfloat16)
        grad_q = jnp.dot(grad_s, key_h, preferred_element_type=jnp.float32) * scaling
        grad_k = (
            jnp.einsum("qk,qe->ke", grad_s, query_h, preferred_element_type=jnp.float32) * scaling
        )
        grad_v = jnp.einsum(
            "qk,qe->ke", probs.astype(jnp.bfloat16), grad_h, preferred_element_type=jnp.float32
        )
        return (grad_q, grad_k, grad_v)

    grads_q, grads_k, grads_v = lax.map(
        one_head,
        (
            split_heads(queries),
            split_heads(keys_all),
            split_heads(values_all),
            split_heads(grad_att),
            log_sums,
        ),
    )
    return (merge_heads(grads_q), merge_heads(grads_k), merge_heads(grads_v))


def mp_total(partial_value):
    rounded = lax.reduce_precision(partial_value, 8, 7)
    other = lax.ppermute(rounded.astype(jnp.bfloat16), "mp", [(0, 1), (1, 0)])
    return rounded + other.astype(jnp.float32)


def axis_bits(mesh):
    bits = []
    for axis in ("dp", "ctx"):
        count = mesh.shape[axis].bit_length() - 1
        bits += [(axis, bit, mesh.shape[axis]) for bit in reversed(range(count))]
    return bits


def step_order(bits, swap):
    low_dp = max(i for i, b in enumerate(bits) if b[0] == "dp")
    ctx_all = [i for i, b in enumerate(bits) if b[0] == "ctx"]
    first = ctx_all + [low_dp] if swap else [low_dp] + ctx_all
    rest = [i for i in reversed(range(len(bits))) if i not in first]
    return first + rest


def my_bit(entry):
    axis, bit, _ = entry
    return (lax.axis_index(axis) >> bit) & 1


def swap_with(value, entry):
    axis, bit, size = entry
    return lax.ppermute(value, axis, [(i, i ^ (1 << bit)) for i in range(size)])


def gather_rows(block, bits, swap):
    held = []
    current = block
    for position in reversed(step_order(bits, swap)):
        entry = bits[position]
        received = swap_with(current, entry)
        mine = my_bit(entry) == 0
        place = sum(1 for h in held if h < position)
        current = jnp.stack(
            [jnp.where(mine, current, received), jnp.where(mine, received, current)], axis=place
        )
        held.append(position)
    return current.reshape(-1, block.shape[-1])


def scatter_rows(total, bits, swap):
    width = total.shape[-1]
    current = total.reshape((2,) * len(bits) + (-1, width))
    left = list(range(len(bits)))
    for position in step_order(bits, swap):
        entry = bits[position]
        place = left.index(position)
        bit = my_bit(entry)
        sent = lax.dynamic_index_in_dim(current, 1 - bit, place, keepdims=False)
        kept = lax.dynamic_index_in_dim(current, bit, place, keepdims=False)
        received = swap_with(sent.astype(jnp.bfloat16), entry)
        current = kept + received.astype(jnp.float32)
        left.remove(position)
    return current


def other_ctx(value, mesh):
    size = mesh.shape["ctx"]
    return lax.ppermute(value, "ctx", [(i, size - 1 - i) for i in range(size)])


def forward_layer(state, weights, biases, gains, shifts, mesh):
    w_qkv, w_out, w_up, w_down = weights
    width = w_out.shape[-1]
    normed, scaled_one, inverse_one = norm_forward(state, gains[0], shifts[0])
    normed_one = normed.astype(jnp.bfloat16)
    project = jnp.dot(normed_one, w_qkv, preferred_element_type=jnp.float32)
    queries = (project[:, :width] + biases[0]).astype(jnp.bfloat16)
    values_local = (project[:, 2 * width :] + biases[1]).astype(jnp.bfloat16)
    local = jnp.concatenate([project[:, width : 2 * width].astype(jnp.bfloat16), values_local], axis=1)
    both = jnp.concatenate([local, other_ctx(local, mesh)], axis=0)
    keys_all, values_all = both[:, :width], both[:, width:]
    mixture, log_sums = attend(queries, keys_all, values_all)
    attended = mixture.astype(jnp.bfloat16)
    partial_value = jnp.einsum("rk,dk->rd", attended, w_out, preferred_element_type=jnp.float32)
    state_one = state + (mp_total(partial_value) + shifts[1])
    normed, scaled_two, inverse_two = norm_forward(state_one, gains[1], shifts[2])
    normed_two = normed.astype(jnp.bfloat16)
    hidden_pre = jnp.dot(
        normed_two, w_up, preferred_element_type=jnp.float32
    ) + biases[2:6].reshape(-1)
    hidden_act = gelu_value(hidden_pre).astype(jnp.bfloat16)
    partial_value = jnp.einsum("rj,dj->rd", hidden_act, w_down, preferred_element_type=jnp.float32)
    state_two = state_one + (mp_total(partial_value) + shifts[3])
    saved = (
        scaled_one, inverse_one, normed_one, queries, keys_all, values_all, attended, log_sums,
        scaled_two, inverse_two, normed_two, hidden_pre, hidden_act,
    )
    return (state_two, saved)


def backward_layer(grad_two, weights, gains, saved, bits, mesh, more):
    w_qkv, w_out, w_up, w_down = weights
    (
        scaled_one, inverse_one, normed_one, queries, keys_all, values_all, attended, log_sums,
        scaled_two, inverse_two, normed_two, hidden_pre, hidden_act,
    ) = saved
    rows = grad_two.shape[0]
    width = w_out.shape[-1]
    grad_y = grad_two.astype(jnp.bfloat16)
    down_bias = jnp.sum(grad_y, axis=0, dtype=jnp.float32)
    grad_act = jnp.dot(grad_y, w_down, preferred_element_type=jnp.float32)
    grad_down = jnp.einsum("rd,rj->dj", grad_y, hidden_act, preferred_element_type=jnp.float32)
    grad_down = scatter_rows(grad_down, bits, False)
    grad_pre = (grad_act * gelu_slope(hidden_pre)).astype(jnp.bfloat16)
    up_bias = jnp.sum(grad_pre, axis=0, dtype=jnp.float32)
    grad_norm = mp_total(
        jnp.einsum("rj,dj->rd", grad_pre, w_up, preferred_element_type=jnp.float32)
    )
    grad_up = jnp.einsum("rd,rj->dj", normed_two, grad_pre, preferred_element_type=jnp.float32)
    grad_up = scatter_rows(grad_up, bits, True)
    grad_in, gain_two, shift_two = norm_backward(grad_norm, scaled_two, inverse_two, gains[1])
    grad_one = grad_two + grad_in
    grad_b = grad_one.astype(jnp.bfloat16)
    out_bias = jnp.sum(grad_b, axis=0, dtype=jnp.float32)
    grad_att = jnp.dot(grad_b, w_out, preferred_element_type=jnp.float32).astype(jnp.bfloat16)
    grad_out = jnp.einsum("rd,rk->dk", grad_b, attended, preferred_element_type=jnp.float32)
    grad_out = scatter_rows(grad_out, bits, False)
    grad_q, grad_k_all, grad_v_all = attend_back(queries, keys_all, values_all, grad_att, log_sums)
    kv_all = jnp.concatenate([grad_k_all, grad_v_all], axis=1)
    kv_sum = kv_all[:rows] + other_ctx(kv_all[rows:].astype(jnp.bfloat16), mesh).astype(jnp.float32)
    grad_stack = jnp.concatenate([grad_q, kv_sum], axis=1).astype(jnp.bfloat16)
    stack_bias = jnp.sum(grad_stack, axis=0, dtype=jnp.float32)
    grad_norm = mp_total(
        jnp.einsum("rc,dc->rd", grad_stack, w_qkv, preferred_element_type=jnp.float32)
    )
    grad_qkv = jnp.einsum("rd,rc->dc", normed_one, grad_stack, preferred_element_type=jnp.float32)
    grad_in, gain_one, shift_one = norm_backward(grad_norm, scaled_one, inverse_one, gains[0])
    grad_zero = grad_one + grad_in
    cols = jnp.concatenate(
        [stack_bias[None, :width], stack_bias[None, 2 * width :], up_bias.reshape(4, width)], axis=0
    )
    rowwise = jnp.stack([gain_one, gain_two, shift_one, out_bias, shift_two, down_bias])
    grad_qkv = scatter_rows(grad_qkv, bits, True)
    return (grad_zero, (grad_qkv, grad_out, grad_up, grad_down), cols, rowwise)


LANES = 128


def pad_lanes(matrix):
    return jnp.pad(matrix, ((0, 0), (0, -matrix.shape[1] % LANES)))


def make_shards(mesh):
    bits = axis_bits(mesh)

    def shards(
        frames_in, qkv_weight, out_weight, up_weight, down_weight,
        col_biases, norm_gains, row_shifts, cotangent,
    ):
        layers, block, _, width = qkv_weight.shape
        members = 2 ** len(bits)
        heads, part = col_biases.shape[2:]
        rowwise = jnp.concatenate([norm_gains, row_shifts], axis=1).reshape(-1, block).T
        per_block = layers * 6 * heads * part
        lanes_cols = -(-per_block // block)
        flat_cols = jnp.pad(col_biases.reshape(-1), (0, lanes_cols * block - per_block))
        small = pad_lanes(jnp.concatenate([rowwise, flat_cols.reshape(block, lanes_cols)], axis=1))
        first_width = 3 * width
        all_weights = []
        for layer in range(layers):
            first = jnp.concatenate(
                [qkv_weight[layer].reshape(block, -1)] + ([small] if layer == 0 else []), axis=1
            )
            full_first = gather_rows(first, bits, False)
            if layer == 0:
                small_all = full_first[:, first_width:]
            full_out = gather_rows(out_weight[layer], bits, True)
            full_up = gather_rows(up_weight[layer].reshape(block, -1), bits, True)
            full_down = gather_rows(down_weight[layer].reshape(block, -1), bits, False)
            all_weights.append((full_first[:, :first_width], full_out, full_up, full_down))
        row_count = layers * 6
        row_params = small_all[:, :row_count].T.astype(jnp.float32).reshape(layers, 6, -1)
        cols = small_all[:, row_count : row_count + lanes_cols].reshape(members, -1)[:, :per_block]
        cols = cols.reshape(members, layers, 6, heads, part).transpose(1, 2, 3, 0, 4)
        cols = cols.reshape(layers, 6, width).astype(jnp.float32)

        state = frames_in.astype(jnp.float32)
        kept = []
        for layer in range(layers):
            state, saved = forward_layer(
                state, all_weights[layer], cols[layer],
                row_params[layer, :2], row_params[layer, 2:], mesh,
            )
            kept.append(saved)
        frames_out = state.astype(jnp.bfloat16)
        grad = cotangent.astype(jnp.float32)
        results = [None] * layers
        cols_parts = [None] * layers
        row_parts = [None] * layers
        for layer in reversed(range(layers)):
            grad, results[layer], cols_parts[layer], row_parts[layer] = backward_layer(
                grad, all_weights[layer], row_params[layer, :2], kept[layer], bits, mesh, None
            )
        row_part = jnp.concatenate(row_parts, axis=0).T
        col_part = jnp.stack(cols_parts).reshape(layers, 6, heads, members, part)
        col_part = col_part.transpose(3, 0, 1, 2, 4).reshape(members, per_block)
        col_part = jnp.pad(col_part, ((0, 0), (0, lanes_cols * block - per_block)))
        small_part = jnp.concatenate([row_part, col_part.reshape(members * block, lanes_cols)], axis=1)
        small_sum = scatter_rows(pad_lanes(small_part), bits, False)
        row_sum = small_sum[:, :row_count].T.reshape(layers, 6, block)
        col_sum = small_sum[:, row_count : row_count + lanes_cols].reshape(-1)[:per_block]
        col_sum = col_sum.reshape(layers, 6, heads, part)

        def stacked(member, shape):
            return jnp.stack([results[layer][member].reshape(shape) for layer in range(layers)])

        return (
            frames_out,
            grad,
            stacked(0, (block, 3, width)),
            stacked(1, (block, width)),
            stacked(2, (block, 4, width)),
            stacked(3, (block, 4, width)),
            col_sum,
            row_sum[:, :2],
            row_sum[:, 2:],
        )

    return shards


def solution(mesh):
    placed = (
        P(("dp", "ctx"), None),
        P(None, ("dp", "ctx"), None, "mp"),
        P(None, ("dp", "ctx"), "mp"),
        P(None, ("dp", "ctx"), None, "mp"),
        P(None, ("dp", "ctx"), None, "mp"),
        P(None, None, "mp", ("dp", "ctx")),
        P(None, None, ("dp", "ctx")),
        P(None, None, ("dp", "ctx")),
        P(("dp", "ctx"), None),
    )
    return jax.shard_map(
        make_shards(mesh),
        mesh=mesh,
        in_specs=placed,
        out_specs=(
            P(("dp", "ctx"), None),
            P(("dp", "ctx"), None),
            P(None, ("dp", "ctx"), None, "mp"),
            P(None, ("dp", "ctx"), "mp"),
            P(None, ("dp", "ctx"), None, "mp"),
            P(None, ("dp", "ctx"), None, "mp"),
            P(None, None, "mp", ("dp", "ctx")),
            P(None, None, ("dp", "ctx")),
            P(None, None, ("dp", "ctx")),
        ),
        check_vma=False,
    )
```

```python
import functools

import jax
import jax.numpy as jnp
from jax import lax
from jax.experimental import pallas as pl
from jax.experimental.pallas import tpu as pltpu
from jax.sharding import PartitionSpec as P

HEAD_DIM = 64
CHUNK = 256
INTERPRET = False


root_half = 0.7071067811865476
inv_root_tau = 0.3989422804014327


def norm_forward(values_in, gain, shift):
    middle = jnp.mean(values_in, axis=-1, keepdims=True)
    centred = values_in - middle
    inverse = lax.rsqrt(jnp.mean(centred * centred, axis=-1, keepdims=True) + 1e-05)
    scaled = centred * inverse
    return (scaled * gain + shift, scaled, inverse)


def norm_backward(grad_out, scaled, inverse, gain):
    gain_part = jnp.sum(grad_out * scaled, axis=0)
    shift_part = jnp.sum(grad_out, axis=0)
    weighted = grad_out * gain
    grad_in = inverse * (
        weighted
        - jnp.mean(weighted, axis=-1, keepdims=True)
        - scaled * jnp.mean(weighted * scaled, axis=-1, keepdims=True)
    )
    return (grad_in, gain_part, shift_part)


def gelu_value(pre_act):
    return 0.5 * pre_act * (1.0 + lax.erf(pre_act * root_half))


def gelu_slope(pre_act):
    return (
        0.5 * (1.0 + lax.erf(pre_act * root_half))
        + pre_act * jnp.exp(-0.5 * pre_act * pre_act) * inv_root_tau
    )


scores_to_exp2 = HEAD_DIM ** (-0.5) * 1.4426950408889634
PAIR = 2 * HEAD_DIM


def one_of_pair(block, which):
    lane = lax.broadcasted_iota(jnp.int32, block.shape, 1)
    return jnp.where((lane >= HEAD_DIM) == (which == 1), block, jnp.zeros_like(block))


def dot_nt(left, right):
    return lax.dot_general(left, right, (((1,), (1,)), ((), ())), preferred_element_type=jnp.float32)


def dot_tn(left, right):
    return lax.dot_general(left, right, (((0,), (0,)), ((), ())), preferred_element_type=jnp.float32)


def dot_nn(left, right):
    return lax.dot_general(left, right, (((1,), (0,)), ((), ())), preferred_element_type=jnp.float32)


def attend_kernel(last, *refs):
    if last:
        q_ref, k_ref, v_ref, mix_in, stat_in, out_ref, stat_ref = refs
    else:
        q_ref, k_ref, v_ref, out_ref, stat_ref = refs
    q, k, v = q_ref[...], k_ref[...], v_ref[...]
    mixes = []
    for which in range(2):
        low, high = which * HEAD_DIM, (which + 1) * HEAD_DIM
        scores = dot_nt(k, one_of_pair(q, which))
        top = jnp.max(scores, axis=0, keepdims=True) * scores_to_exp2
        if last:
            old_top = stat_in[which : which + 1, :]
            top = jnp.maximum(top, old_top)
        weights = jnp.exp2(scores * scores_to_exp2 - top)
        total = jnp.sum(weights, axis=0, keepdims=True)
        mix = dot_tn(v, weights.astype(jnp.bfloat16))[low:high, :]
        if last:
            decay = jnp.exp2(old_top - top)
            total = total + decay * stat_in[2 + which : 3 + which, :]
            mix = (mix + decay * mix_in[low:high, :]) / total
            stat_ref[which : which + 1, :] = top + jnp.log2(total)
        else:
            stat_ref[which : which + 1, :] = top
            stat_ref[2 + which : 3 + which, :] = total
        mixes.append(mix)
    mix = jnp.concatenate(mixes, axis=0)
    if last:
        out_ref[...] = mix.T.astype(jnp.bfloat16)
    else:
        out_ref[...] = mix


def chunk_of(rows):
    return CHUNK if rows % CHUNK == 0 else rows


def attend_half(queries, keys_values, carried):
    rows, width = queries.shape
    keys = keys_values.shape[0]
    pairs = width // PAIR
    chunk = chunk_of(rows)
    last = carried is not None
    mix_spec = pl.BlockSpec((None, PAIR, chunk), lambda p, c: (p, 0, c))
    stat_spec = pl.BlockSpec((None, 8, chunk), lambda p, c: (p, 0, c))
    stat_shape = jax.ShapeDtypeStruct((pairs, 8, rows), jnp.float32)
    q_spec = pl.BlockSpec((chunk, PAIR), lambda p, c: (c, p))
    in_specs = [
        q_spec,
        pl.BlockSpec((keys, PAIR), lambda p, c: (0, p)),
        pl.BlockSpec((keys, PAIR), lambda p, c: (0, p + pairs)),
    ]
    args = (queries, keys_values, keys_values)
    if last:
        in_specs += [mix_spec, stat_spec]
        args += tuple(carried)
        out = jax.ShapeDtypeStruct((rows, width), jnp.bfloat16)
    else:
        out = jax.ShapeDtypeStruct((pairs, PAIR, rows), jnp.float32)
    return pl.pallas_call(
        functools.partial(attend_kernel, last),
        grid=(pairs, rows // chunk),
        in_specs=in_specs,
        out_specs=(q_spec if last else mix_spec, stat_spec),
        out_shape=(out, stat_shape),
        cost_estimate=pl.CostEstimate(
            flops=4 * rows * keys * width * 4,
            transcendentals=rows * keys * 2 * pairs,
            bytes_accessed=rows * width * 12,
        ),
        interpret=INTERPRET,
        name="attend_last" if last else "attend_first",
    )(*args)


def attend_back_kernel(q_ref, k_ref, v_ref, g_ref, o_ref, stat_ref, dq_ref, dkv_ref, acc_ref):
    step = pl.program_id(1)
    q, k, v, g = q_ref[...], k_ref[...], v_ref[...], g_ref[...]
    inner_all = (g.astype(jnp.float32) * o_ref[...].astype(jnp.float32)).T
    dq = None
    for which in range(2):
        low, high = which * HEAD_DIM, (which + 1) * HEAD_DIM
        q_one, g_one = one_of_pair(q, which), one_of_pair(g, which)
        inner = jnp.sum(inner_all[low:high, :], axis=0, keepdims=True)
        probs = jnp.exp2(dot_nt(k, q_one) * scores_to_exp2 - stat_ref[which : which + 1, :])
        grad_p = dot_nt(v, g_one)
        grad_s = (probs * (grad_p - inner)).astype(jnp.bfloat16)
        dv_part = dot_nn(probs.astype(jnp.bfloat16), g_one)
        dk_part = dot_nn(grad_s, q_one)
        dq_part = dot_tn(one_of_pair(k, which), grad_s)
        if which == 0:
            dv, dk, dq = dv_part, dk_part, dq_part
        else:
            dv, dk, dq = dv + dv_part, dk + dk_part, dq + dq_part
    scaling = HEAD_DIM ** (-0.5)
    dq_ref[...] = dq.T * scaling
    both = jnp.stack([dk * scaling, dv])

    @pl.when(step == 0)
    def _():
        acc_ref[...] = both

    @pl.when(step > 0)
    def _():
        acc_ref[...] += both

    @pl.when(step == pl.num_programs(1) - 1)
    def _():
        dkv_ref[...] = acc_ref[...].astype(dkv_ref.dtype)


def attend_back_half(queries, keys_values, grad_att, attended, stats, kind):
    rows, width = queries.shape
    keys = keys_values.shape[0]
    pairs = width // PAIR
    chunk = chunk_of(rows)
    q_spec = pl.BlockSpec((chunk, PAIR), lambda p, c: (c, p))
    return pl.pallas_call(
        attend_back_kernel,
        grid=(pairs, rows // chunk),
        in_specs=[
            q_spec,
            pl.BlockSpec((keys, PAIR), lambda p, c: (0, p)),
            pl.BlockSpec((keys, PAIR), lambda p, c: (0, p + pairs)),
            q_spec,
            q_spec,
            pl.BlockSpec((None, 8, chunk), lambda p, c: (p, 0, c)),
        ],
        out_specs=(q_spec, pl.BlockSpec((2, keys, PAIR), lambda p, c: (0, 0, p))),
        out_shape=(
            jax.ShapeDtypeStruct((rows, width), jnp.float32),
            jax.ShapeDtypeStruct((2, keys, width), kind),
        ),
        scratch_shapes=[pltpu.VMEM((2, keys, PAIR), jnp.float32)],
        cost_estimate=pl.CostEstimate(
            flops=10 * rows * keys * width * 4,
            transcendentals=rows * keys * 2 * pairs,
            bytes_accessed=rows * width * 24,
        ),
        interpret=INTERPRET,
        name="attend_back",
    )(queries, keys_values, keys_values, grad_att, attended, stats)


def mp_total(partial_value):
    rounded = lax.reduce_precision(partial_value, 8, 7)
    other = lax.ppermute(rounded.astype(jnp.bfloat16), "mp", [(0, 1), (1, 0)])
    return rounded + other.astype(jnp.float32)


def axis_bits(mesh):
    bits = []
    for axis in ("dp", "ctx"):
        count = mesh.shape[axis].bit_length() - 1
        bits += [(axis, bit, mesh.shape[axis]) for bit in reversed(range(count))]
    return bits


def step_order(bits, swap):
    low_dp = max(i for i, b in enumerate(bits) if b[0] == "dp")
    ctx_all = [i for i, b in enumerate(bits) if b[0] == "ctx"]
    first = ctx_all + [low_dp] if swap else [low_dp] + ctx_all
    rest = [i for i in reversed(range(len(bits))) if i not in first]
    return first + rest


def my_bit(entry):
    axis, bit, _ = entry
    return (lax.axis_index(axis) >> bit) & 1


def swap_with(value, entry):
    axis, bit, size = entry
    return lax.ppermute(value, axis, [(i, i ^ (1 << bit)) for i in range(size)])


def gather_rows(block, bits, swap, after=None):
    held = []
    if after is not None:
        block, _ = lax.optimization_barrier((block, after))
    current = block
    for position in reversed(step_order(bits, swap)):
        entry = bits[position]
        received = swap_with(current, entry)
        mine = my_bit(entry) == 0
        place = sum(1 for h in held if h < position)
        current = jnp.stack(
            [jnp.where(mine, current, received), jnp.where(mine, received, current)], axis=place
        )
        held.append(position)
    return current.reshape(-1, block.shape[-1]), received


def scatter_rows(total, bits, swap):
    width = total.shape[-1]
    current = total.reshape((2,) * len(bits) + (-1, width))
    left = list(range(len(bits)))
    for position in step_order(bits, swap):
        entry = bits[position]
        place = left.index(position)
        bit = my_bit(entry)
        sent = lax.dynamic_index_in_dim(current, 1 - bit, place, keepdims=False)
        kept = lax.dynamic_index_in_dim(current, bit, place, keepdims=False)
        received = swap_with(sent.astype(jnp.bfloat16), entry)
        current = kept + received.astype(jnp.float32)
        left.remove(position)
    return current


def other_ctx(value, mesh):
    size = mesh.shape["ctx"]
    return lax.ppermute(value, "ctx", [(i, size - 1 - i) for i in range(size)])


def forward_layer(state, weights, biases, gains, shifts, mesh):
    w_q, w_kv, w_out, w_up, w_down = weights
    width = w_out.shape[-1]
    normed, scaled_one, inverse_one = norm_forward(state, gains[0], shifts[0])
    normed_one = normed.astype(jnp.bfloat16)
    project = jnp.dot(normed_one, w_kv, preferred_element_type=jnp.float32)
    kv_bias = jnp.concatenate([jnp.zeros_like(biases[1]), biases[1]])
    near = (project + kv_bias).astype(jnp.bfloat16)
    far = other_ctx(near, mesh)
    queries = jnp.dot(normed_one, w_q, preferred_element_type=jnp.float32) + biases[0]
    queries = queries.astype(jnp.bfloat16)
    carried = attend_half(queries, near, None)
    attended, stats = attend_half(queries, far, carried)
    partial_value = jnp.einsum("rk,dk->rd", attended, w_out, preferred_element_type=jnp.float32)
    state_one = state + (mp_total(partial_value) + shifts[1])
    normed, scaled_two, inverse_two = norm_forward(state_one, gains[1], shifts[2])
    normed_two = normed.astype(jnp.bfloat16)
    hidden_pre = jnp.dot(
        normed_two, w_up, preferred_element_type=jnp.float32
    ) + biases[2:6].reshape(-1)
    hidden_act = gelu_value(hidden_pre).astype(jnp.bfloat16)
    partial_value = jnp.einsum("rj,dj->rd", hidden_act, w_down, preferred_element_type=jnp.float32)
    state_two = state_one + (mp_total(partial_value) + shifts[3])
    saved = (
        scaled_one, inverse_one, normed_one, queries, near, far, attended, stats,
        scaled_two, inverse_two, normed_two, hidden_pre, hidden_act,
    )
    return (state_two, saved)


def backward_layer(grad_two, weights, gains, saved, bits, mesh, more):
    w_q, w_kv, w_out, w_up, w_down = weights
    (
        scaled_one, inverse_one, normed_one, queries, near, far, attended, stats,
        scaled_two, inverse_two, normed_two, hidden_pre, hidden_act,
    ) = saved
    width = w_out.shape[-1]
    grad_y = grad_two.astype(jnp.bfloat16)
    down_bias = jnp.sum(grad_y, axis=0, dtype=jnp.float32)
    grad_act = jnp.dot(grad_y, w_down, preferred_element_type=jnp.float32)
    grad_down = jnp.einsum("rd,rj->dj", grad_y, hidden_act, preferred_element_type=jnp.float32)
    grad_down = scatter_rows(grad_down, bits, False)
    grad_pre = (grad_act * gelu_slope(hidden_pre)).astype(jnp.bfloat16)
    up_bias = jnp.sum(grad_pre, axis=0, dtype=jnp.float32)
    grad_norm = mp_total(
        jnp.einsum("rj,dj->rd", grad_pre, w_up, preferred_element_type=jnp.float32)
    )
    grad_up = jnp.einsum("rd,rj->dj", normed_two, grad_pre, preferred_element_type=jnp.float32)
    grad_up = scatter_rows(grad_up, bits, True)
    grad_in, gain_two, shift_two = norm_backward(grad_norm, scaled_two, inverse_two, gains[1])
    grad_one = grad_two + grad_in
    grad_b = grad_one.astype(jnp.bfloat16)
    out_bias = jnp.sum(grad_b, axis=0, dtype=jnp.float32)
    grad_att = jnp.dot(grad_b, w_out, preferred_element_type=jnp.float32).astype(jnp.bfloat16)
    grad_out = jnp.einsum("rd,rk->dk", grad_b, attended, preferred_element_type=jnp.float32)
    grad_out = scatter_rows(grad_out, bits, False)
    dq_far, dkv_far = attend_back_half(
        queries, far, grad_att, attended, stats, jnp.bfloat16
    )
    returned = other_ctx(dkv_far, mesh)
    grad_att, dq_far = lax.optimization_barrier((grad_att, dq_far))
    dq_near, dkv_near = attend_back_half(
        queries, near, grad_att, attended, stats, jnp.float32
    )
    grad_q = (dq_far + dq_near).astype(jnp.bfloat16)
    dkv = (dkv_near + returned.astype(jnp.float32)).astype(jnp.bfloat16)
    grad_kv = jnp.concatenate([dkv[0], dkv[1]], axis=1)
    query_bias = jnp.sum(grad_q, axis=0, dtype=jnp.float32)
    value_bias = jnp.sum(dkv[1], axis=0, dtype=jnp.float32)
    grad_norm = mp_total(
        jnp.einsum("rc,dc->rd", grad_q, w_q, preferred_element_type=jnp.float32)
        + jnp.einsum("rc,dc->rd", grad_kv, w_kv, preferred_element_type=jnp.float32)
    )
    grad_wq = jnp.einsum("rd,rc->dc", normed_one, grad_q, preferred_element_type=jnp.float32)
    grad_wkv = jnp.einsum("rd,rc->dc", normed_one, grad_kv, preferred_element_type=jnp.float32)
    grad_wkv = scatter_rows(grad_wkv, bits, False)
    grad_wq = scatter_rows(grad_wq, bits, True)
    grad_qkv = jnp.concatenate([grad_wq, grad_wkv], axis=1)
    grad_in, gain_one, shift_one = norm_backward(grad_norm, scaled_one, inverse_one, gains[0])
    grad_zero = grad_one + grad_in
    cols = jnp.concatenate(
        [query_bias[None], value_bias[None], up_bias.reshape(4, width)], axis=0
    )
    rowwise = jnp.stack([gain_one, gain_two, shift_one, out_bias, shift_two, down_bias])
    return (grad_zero, (grad_qkv, grad_out, grad_up, grad_down), cols, rowwise)


LANES = 128


def pad_lanes(matrix):
    return jnp.pad(matrix, ((0, 0), (0, -matrix.shape[1] % LANES)))


def make_shards(mesh):
    bits = axis_bits(mesh)

    def shards(
        frames_in, qkv_weight, out_weight, up_weight, down_weight,
        col_biases, norm_gains, row_shifts, cotangent,
    ):
        layers, block, _, width = qkv_weight.shape
        members = 2 ** len(bits)
        heads, part = col_biases.shape[2:]
        rowwise = jnp.concatenate([norm_gains, row_shifts], axis=1).reshape(-1, block).T
        per_block = layers * 6 * heads * part
        lanes_cols = -(-per_block // block)
        flat_cols = jnp.pad(col_biases.reshape(-1), (0, lanes_cols * block - per_block))
        small = pad_lanes(jnp.concatenate([rowwise, flat_cols.reshape(block, lanes_cols)], axis=1))
        pieces = []
        for layer in range(layers):
            qkv_rows = qkv_weight[layer].reshape(block, -1)
            query_rows = qkv_rows[:, :width]
            if layer == 0:
                query_rows = jnp.concatenate([query_rows, small], axis=1)
            pieces += [
                query_rows, qkv_rows[:, width:], out_weight[layer],
                up_weight[layer].reshape(block, -1), down_weight[layer].reshape(block, -1),
            ]
        full, tokens = [], []
        for which, piece in enumerate(pieces):
            after = tokens[which - 2] if which > 1 else None
            gathered, token = gather_rows(piece, bits, which % 2 == 0, after)
            full.append(gathered)
            tokens.append(token)
        small_all = full[0][:, width:]
        full[0] = full[0][:, :width]
        all_weights = [tuple(full[5 * layer : 5 * layer + 5]) for layer in range(layers)]
        row_count = layers * 6
        row_params = small_all[:, :row_count].T.astype(jnp.float32).reshape(layers, 6, -1)
        cols = small_all[:, row_count : row_count + lanes_cols].reshape(members, -1)[:, :per_block]
        cols = cols.reshape(members, layers, 6, heads, part).transpose(1, 2, 3, 0, 4)
        cols = cols.reshape(layers, 6, width).astype(jnp.float32)

        state = frames_in.astype(jnp.float32)
        kept = []
        for layer in range(layers):
            state, saved = forward_layer(
                state, all_weights[layer], cols[layer],
                row_params[layer, :2], row_params[layer, 2:], mesh,
            )
            kept.append(saved)
        frames_out = state.astype(jnp.bfloat16)
        grad = cotangent.astype(jnp.float32)
        results = [None] * layers
        cols_parts = [None] * layers
        row_parts = [None] * layers
        for layer in reversed(range(layers)):
            grad, results[layer], cols_parts[layer], row_parts[layer] = backward_layer(
                grad, all_weights[layer], row_params[layer, :2], kept[layer], bits, mesh, None
            )
        row_part = jnp.concatenate(row_parts, axis=0).T
        col_part = jnp.stack(cols_parts).reshape(layers, 6, heads, members, part)
        col_part = col_part.transpose(3, 0, 1, 2, 4).reshape(members, per_block)
        col_part = jnp.pad(col_part, ((0, 0), (0, lanes_cols * block - per_block)))
        small_part = jnp.concatenate([row_part, col_part.reshape(members * block, lanes_cols)], axis=1)
        small_sum = scatter_rows(pad_lanes(small_part), bits, False)
        row_sum = small_sum[:, :row_count].T.reshape(layers, 6, block)
        col_sum = small_sum[:, row_count : row_count + lanes_cols].reshape(-1)[:per_block]
        col_sum = col_sum.reshape(layers, 6, heads, part)

        def stacked(member, shape):
            return jnp.stack([results[layer][member].reshape(shape) for layer in range(layers)])

        return (
            frames_out,
            grad,
            stacked(0, (block, 3, width)),
            stacked(1, (block, width)),
            stacked(2, (block, 4, width)),
            stacked(3, (block, 4, width)),
            col_sum,
            row_sum[:, :2],
            row_sum[:, 2:],
        )

    return shards


def solution(mesh):
    placed = (
        P(("dp", "ctx"), None),
        P(None, ("dp", "ctx"), None, "mp"),
        P(None, ("dp", "ctx"), "mp"),
        P(None, ("dp", "ctx"), None, "mp"),
        P(None, ("dp", "ctx"), None, "mp"),
        P(None, None, "mp", ("dp", "ctx")),
        P(None, None, ("dp", "ctx")),
        P(None, None, ("dp", "ctx")),
        P(("dp", "ctx"), None),
    )
    return jax.shard_map(
        make_shards(mesh),
        mesh=mesh,
        in_specs=placed,
        out_specs=(
            P(("dp", "ctx"), None),
            P(("dp", "ctx"), None),
            P(None, ("dp", "ctx"), None, "mp"),
            P(None, ("dp", "ctx"), "mp"),
            P(None, ("dp", "ctx"), None, "mp"),
            P(None, ("dp", "ctx"), None, "mp"),
            P(None, None, "mp", ("dp", "ctx")),
            P(None, None, ("dp", "ctx")),
            P(None, None, ("dp", "ctx")),
        ),
        check_vma=False,
    )
```

```python
import functools

import jax
import jax.numpy as jnp
from jax import lax
from jax.experimental import pallas as pl
from jax.experimental.pallas import tpu as pltpu
from jax.sharding import PartitionSpec as P

HEAD_DIM = 64
CHUNK = 256
INTERPRET = False


root_half = 0.7071067811865476
inv_root_tau = 0.3989422804014327


def norm_forward(values_in, gain, shift):
    middle = jnp.mean(values_in, axis=-1, keepdims=True)
    centred = values_in - middle
    inverse = lax.rsqrt(jnp.mean(centred * centred, axis=-1, keepdims=True) + 1e-05)
    scaled = centred * inverse
    return (scaled * gain + shift, scaled, inverse)


def norm_backward(grad_out, scaled, inverse, gain):
    gain_part = jnp.sum(grad_out * scaled, axis=0)
    shift_part = jnp.sum(grad_out, axis=0)
    weighted = grad_out * gain
    grad_in = inverse * (
        weighted
        - jnp.mean(weighted, axis=-1, keepdims=True)
        - scaled * jnp.mean(weighted * scaled, axis=-1, keepdims=True)
    )
    return (grad_in, gain_part, shift_part)


def gelu_value(pre_act):
    return 0.5 * pre_act * (1.0 + lax.erf(pre_act * root_half))


def gelu_slope(pre_act):
    return (
        0.5 * (1.0 + lax.erf(pre_act * root_half))
        + pre_act * jnp.exp(-0.5 * pre_act * pre_act) * inv_root_tau
    )


scores_to_exp2 = HEAD_DIM ** (-0.5) * 1.4426950408889634
PAIR = 2 * HEAD_DIM


def one_of_pair(block, which):
    lane = lax.broadcasted_iota(jnp.int32, block.shape, 1)
    return jnp.where((lane >= HEAD_DIM) == (which == 1), block, jnp.zeros_like(block))


def dot_nt(left, right):
    return lax.dot_general(left, right, (((1,), (1,)), ((), ())), preferred_element_type=jnp.float32)


def dot_tn(left, right):
    return lax.dot_general(left, right, (((0,), (0,)), ((), ())), preferred_element_type=jnp.float32)


def dot_nn(left, right):
    return lax.dot_general(left, right, (((1,), (0,)), ((), ())), preferred_element_type=jnp.float32)


def attend_kernel(last, *refs):
    if last:
        q_ref, k_ref, v_ref, mix_in, stat_in, out_ref, stat_ref = refs
    else:
        q_ref, k_ref, v_ref, out_ref, stat_ref = refs
    q, k, v = q_ref[...], k_ref[...], v_ref[...]
    mixes = []
    for which in range(2):
        low, high = which * HEAD_DIM, (which + 1) * HEAD_DIM
        scores = dot_nt(k, one_of_pair(q, which))
        top = jnp.max(scores, axis=0, keepdims=True) * scores_to_exp2
        if last:
            old_top = stat_in[which : which + 1, :]
            top = jnp.maximum(top, old_top)
        weights = jnp.exp2(scores * scores_to_exp2 - top)
        total = jnp.sum(weights, axis=0, keepdims=True)
        mix = dot_tn(v, weights.astype(jnp.bfloat16))[low:high, :]
        if last:
            decay = jnp.exp2(old_top - top)
            total = total + decay * stat_in[2 + which : 3 + which, :]
            mix = (mix + decay * mix_in[low:high, :]) / total
            stat_ref[which : which + 1, :] = top + jnp.log2(total)
        else:
            stat_ref[which : which + 1, :] = top
            stat_ref[2 + which : 3 + which, :] = total
        mixes.append(mix)
    mix = jnp.concatenate(mixes, axis=0)
    if last:
        out_ref[...] = mix.T.astype(jnp.bfloat16)
    else:
        out_ref[...] = mix


def chunk_of(rows):
    return CHUNK if rows % CHUNK == 0 else rows


def attend_half(queries, keys_values, carried):
    rows, width = queries.shape
    keys = keys_values.shape[0]
    pairs = width // PAIR
    chunk = chunk_of(rows)
    last = carried is not None
    mix_spec = pl.BlockSpec((None, PAIR, chunk), lambda p, c: (p, 0, c))
    stat_spec = pl.BlockSpec((None, 8, chunk), lambda p, c: (p, 0, c))
    stat_shape = jax.ShapeDtypeStruct((pairs, 8, rows), jnp.float32)
    q_spec = pl.BlockSpec((chunk, PAIR), lambda p, c: (c, p))
    in_specs = [
        q_spec,
        pl.BlockSpec((keys, PAIR), lambda p, c: (0, p)),
        pl.BlockSpec((keys, PAIR), lambda p, c: (0, p + pairs)),
    ]
    args = (queries, keys_values, keys_values)
    if last:
        in_specs += [mix_spec, stat_spec]
        args += tuple(carried)
        out = jax.ShapeDtypeStruct((rows, width), jnp.bfloat16)
    else:
        out = jax.ShapeDtypeStruct((pairs, PAIR, rows), jnp.float32)
    return pl.pallas_call(
        functools.partial(attend_kernel, last),
        grid=(pairs, rows // chunk),
        in_specs=in_specs,
        out_specs=(q_spec if last else mix_spec, stat_spec),
        out_shape=(out, stat_shape),
        cost_estimate=pl.CostEstimate(
            flops=4 * rows * keys * width * 4,
            transcendentals=rows * keys * 2 * pairs,
            bytes_accessed=rows * width * 12,
        ),
        interpret=INTERPRET,
        name="attend_last" if last else "attend_first",
    )(*args)


def attend_back_kernel(q_ref, k_ref, v_ref, g_ref, o_ref, stat_ref, dq_ref, dkv_ref, acc_ref):
    step = pl.program_id(1)
    q, k, v, g = q_ref[...], k_ref[...], v_ref[...], g_ref[...]
    inner_all = (g.astype(jnp.float32) * o_ref[...].astype(jnp.float32)).T
    dq = None
    for which in range(2):
        low, high = which * HEAD_DIM, (which + 1) * HEAD_DIM
        q_one, g_one = one_of_pair(q, which), one_of_pair(g, which)
        inner = jnp.sum(inner_all[low:high, :], axis=0, keepdims=True)
        probs = jnp.exp2(dot_nt(k, q_one) * scores_to_exp2 - stat_ref[which : which + 1, :])
        grad_p = dot_nt(v, g_one)
        grad_s = (probs * (grad_p - inner)).astype(jnp.bfloat16)
        dv_part = dot_nn(probs.astype(jnp.bfloat16), g_one)
        dk_part = dot_nn(grad_s, q_one)
        dq_part = dot_tn(one_of_pair(k, which), grad_s)
        if which == 0:
            dv, dk, dq = dv_part, dk_part, dq_part
        else:
            dv, dk, dq = dv + dv_part, dk + dk_part, dq + dq_part
    scaling = HEAD_DIM ** (-0.5)
    dq_ref[...] = dq.T * scaling
    both = jnp.stack([dk * scaling, dv])

    @pl.when(step == 0)
    def _():
        acc_ref[...] = both

    @pl.when(step > 0)
    def _():
        acc_ref[...] += both

    @pl.when(step == pl.num_programs(1) - 1)
    def _():
        dkv_ref[...] = acc_ref[...].astype(dkv_ref.dtype)


def attend_back_half(queries, keys_values, grad_att, attended, stats, kind):
    rows, width = queries.shape
    keys = keys_values.shape[0]
    pairs = width // PAIR
    chunk = chunk_of(rows)
    q_spec = pl.BlockSpec((chunk, PAIR), lambda p, c: (c, p))
    return pl.pallas_call(
        attend_back_kernel,
        grid=(pairs, rows // chunk),
        in_specs=[
            q_spec,
            pl.BlockSpec((keys, PAIR), lambda p, c: (0, p)),
            pl.BlockSpec((keys, PAIR), lambda p, c: (0, p + pairs)),
            q_spec,
            q_spec,
            pl.BlockSpec((None, 8, chunk), lambda p, c: (p, 0, c)),
        ],
        out_specs=(q_spec, pl.BlockSpec((2, keys, PAIR), lambda p, c: (0, 0, p))),
        out_shape=(
            jax.ShapeDtypeStruct((rows, width), jnp.float32),
            jax.ShapeDtypeStruct((2, keys, width), kind),
        ),
        scratch_shapes=[pltpu.VMEM((2, keys, PAIR), jnp.float32)],
        cost_estimate=pl.CostEstimate(
            flops=10 * rows * keys * width * 4,
            transcendentals=rows * keys * 2 * pairs,
            bytes_accessed=rows * width * 24,
        ),
        interpret=INTERPRET,
        name="attend_back",
    )(queries, keys_values, keys_values, grad_att, attended, stats)


def mp_total(partial_value):
    rounded = lax.reduce_precision(partial_value, 8, 7)
    other = lax.ppermute(rounded.astype(jnp.bfloat16), "mp", [(0, 1), (1, 0)])
    return rounded + other.astype(jnp.float32)


def axis_bits(mesh):
    bits = []
    for axis in ("dp", "ctx"):
        count = mesh.shape[axis].bit_length() - 1
        bits += [(axis, bit, mesh.shape[axis]) for bit in reversed(range(count))]
    return bits


def step_order(bits, swap):
    low_dp = max(i for i, b in enumerate(bits) if b[0] == "dp")
    ctx_all = [i for i, b in enumerate(bits) if b[0] == "ctx"]
    first = ctx_all + [low_dp] if swap else [low_dp] + ctx_all
    rest = [i for i in reversed(range(len(bits))) if i not in first]
    return first + rest


def my_bit(entry):
    axis, bit, _ = entry
    return (lax.axis_index(axis) >> bit) & 1


def swap_with(value, entry):
    axis, bit, size = entry
    return lax.ppermute(value, axis, [(i, i ^ (1 << bit)) for i in range(size)])


def gather_rows(block, bits, swap, after=None):
    held = []
    if after is not None:
        block, _ = lax.optimization_barrier((block, after))
    current = block
    for position in reversed(step_order(bits, swap)):
        entry = bits[position]
        received = swap_with(current, entry)
        mine = my_bit(entry) == 0
        place = sum(1 for h in held if h < position)
        current = jnp.stack(
            [jnp.where(mine, current, received), jnp.where(mine, received, current)], axis=place
        )
        held.append(position)
    return current.reshape(-1, block.shape[-1]), received


def scatter_rows(total, bits, swap):
    width = total.shape[-1]
    current = total.reshape((2,) * len(bits) + (-1, width))
    left = list(range(len(bits)))
    for position in step_order(bits, swap):
        entry = bits[position]
        place = left.index(position)
        bit = my_bit(entry)
        sent = lax.dynamic_index_in_dim(current, 1 - bit, place, keepdims=False)
        kept = lax.dynamic_index_in_dim(current, bit, place, keepdims=False)
        received = swap_with(sent.astype(jnp.bfloat16), entry)
        current = kept + received.astype(jnp.float32)
        left.remove(position)
    return current


def other_ctx(value, mesh):
    size = mesh.shape["ctx"]
    return lax.ppermute(value, "ctx", [(i, size - 1 - i) for i in range(size)])


def forward_layer(state, weights, biases, gains, shifts, mesh):
    w_q, w_kv, w_out, w_up, w_down = weights
    width = w_out.shape[-1]
    normed, scaled_one, inverse_one = norm_forward(state, gains[0], shifts[0])
    normed_one = normed.astype(jnp.bfloat16)
    project = jnp.dot(normed_one, w_kv, preferred_element_type=jnp.float32)
    kv_bias = jnp.concatenate([jnp.zeros_like(biases[1]), biases[1]])
    near = (project + kv_bias).astype(jnp.bfloat16)
    far = other_ctx(near, mesh)
    queries = jnp.dot(normed_one, w_q, preferred_element_type=jnp.float32) + biases[0]
    queries = queries.astype(jnp.bfloat16)
    carried = attend_half(queries, near, None)
    attended, stats = attend_half(queries, far, carried)
    partial_value = jnp.einsum("rk,dk->rd", attended, w_out, preferred_element_type=jnp.float32)
    state_one = state + (mp_total(partial_value) + shifts[1])
    normed, scaled_two, inverse_two = norm_forward(state_one, gains[1], shifts[2])
    normed_two = normed.astype(jnp.bfloat16)
    hidden_pre = jnp.dot(
        normed_two, w_up, preferred_element_type=jnp.float32
    ) + biases[2:6].reshape(-1)
    hidden_act = gelu_value(hidden_pre).astype(jnp.bfloat16)
    partial_value = jnp.einsum("rj,dj->rd", hidden_act, w_down, preferred_element_type=jnp.float32)
    state_two = state_one + (mp_total(partial_value) + shifts[3])
    saved = (
        scaled_one, inverse_one, normed_one, queries, near, far, attended, stats,
        scaled_two, inverse_two, normed_two, hidden_pre, hidden_act,
    )
    return (state_two, saved)


def backward_layer(grad_two, weights, gains, saved, bits, mesh, more):
    w_q, w_kv, w_out, w_up, w_down = weights
    (
        scaled_one, inverse_one, normed_one, queries, near, far, attended, stats,
        scaled_two, inverse_two, normed_two, hidden_pre, hidden_act,
    ) = saved
    width = w_out.shape[-1]
    grad_y = grad_two.astype(jnp.bfloat16)
    down_bias = jnp.sum(grad_y, axis=0, dtype=jnp.float32)
    grad_act = jnp.dot(grad_y, w_down, preferred_element_type=jnp.float32)
    grad_down = jnp.einsum("rd,rj->dj", grad_y, hidden_act, preferred_element_type=jnp.float32)
    grad_down = scatter_rows(grad_down, bits, False)
    grad_pre = (grad_act * gelu_slope(hidden_pre)).astype(jnp.bfloat16)
    up_bias = jnp.sum(grad_pre, axis=0, dtype=jnp.float32)
    grad_norm = mp_total(
        jnp.einsum("rj,dj->rd", grad_pre, w_up, preferred_element_type=jnp.float32)
    )
    grad_up = jnp.einsum("rd,rj->dj", normed_two, grad_pre, preferred_element_type=jnp.float32)
    grad_up = scatter_rows(grad_up, bits, True)
    grad_in, gain_two, shift_two = norm_backward(grad_norm, scaled_two, inverse_two, gains[1])
    grad_one = grad_two + grad_in
    grad_b = grad_one.astype(jnp.bfloat16)
    out_bias = jnp.sum(grad_b, axis=0, dtype=jnp.float32)
    grad_att = jnp.dot(grad_b, w_out, preferred_element_type=jnp.float32).astype(jnp.bfloat16)
    grad_out = jnp.einsum("rd,rk->dk", grad_b, attended, preferred_element_type=jnp.float32)
    grad_out = scatter_rows(grad_out, bits, False)
    dq_far, dkv_far = attend_back_half(
        queries, far, grad_att, attended, stats, jnp.bfloat16
    )
    returned = other_ctx(dkv_far, mesh)
    grad_att, dq_far = lax.optimization_barrier((grad_att, dq_far))
    dq_near, dkv_near = attend_back_half(
        queries, near, grad_att, attended, stats, jnp.float32
    )
    grad_q = (dq_far + dq_near).astype(jnp.bfloat16)
    dkv = (dkv_near + returned.astype(jnp.float32)).astype(jnp.bfloat16)
    grad_kv = jnp.concatenate([dkv[0], dkv[1]], axis=1)
    query_bias = jnp.sum(grad_q, axis=0, dtype=jnp.float32)
    value_bias = jnp.sum(dkv[1], axis=0, dtype=jnp.float32)
    grad_norm = mp_total(
        jnp.einsum("rc,dc->rd", grad_q, w_q, preferred_element_type=jnp.float32)
        + jnp.einsum("rc,dc->rd", grad_kv, w_kv, preferred_element_type=jnp.float32)
    )
    grad_wq = jnp.einsum("rd,rc->dc", normed_one, grad_q, preferred_element_type=jnp.float32)
    grad_wkv = jnp.einsum("rd,rc->dc", normed_one, grad_kv, preferred_element_type=jnp.float32)
    grad_wkv = scatter_rows(grad_wkv, bits, False)
    grad_wq = scatter_rows(grad_wq, bits, True)
    grad_qkv = jnp.concatenate([grad_wq, grad_wkv], axis=1)
    grad_in, gain_one, shift_one = norm_backward(grad_norm, scaled_one, inverse_one, gains[0])
    grad_zero = grad_one + grad_in
    cols = jnp.concatenate(
        [query_bias[None], value_bias[None], up_bias.reshape(4, width)], axis=0
    )
    rowwise = jnp.stack([gain_one, gain_two, shift_one, out_bias, shift_two, down_bias])
    return (grad_zero, (grad_qkv, grad_out, grad_up, grad_down), cols, rowwise)


LANES = 128


def pad_lanes(matrix):
    return jnp.pad(matrix, ((0, 0), (0, -matrix.shape[1] % LANES)))


def make_shards(mesh):
    bits = axis_bits(mesh)

    def shards(
        frames_in, qkv_weight, out_weight, up_weight, down_weight,
        col_biases, norm_gains, row_shifts, cotangent,
    ):
        layers, block, _, width = qkv_weight.shape
        members = 2 ** len(bits)
        heads, part = col_biases.shape[2:]
        rowwise = jnp.concatenate([norm_gains, row_shifts], axis=1).reshape(-1, block).T
        per_block = layers * 6 * heads * part
        lanes_cols = -(-per_block // block)
        flat_cols = jnp.pad(col_biases.reshape(-1), (0, lanes_cols * block - per_block))
        small = pad_lanes(jnp.concatenate([rowwise, flat_cols.reshape(block, lanes_cols)], axis=1))
        pieces = []
        for layer in range(layers):
            qkv_rows = qkv_weight[layer].reshape(block, -1)
            query_rows = qkv_rows[:, :width]
            if layer == 0:
                query_rows = jnp.concatenate([query_rows, small], axis=1)
            pieces += [
                query_rows, qkv_rows[:, width:], out_weight[layer],
                up_weight[layer].reshape(block, -1), down_weight[layer].reshape(block, -1),
            ]
        full, tokens = [], []
        for which, piece in enumerate(pieces):
            after = None if which < 2 else tokens[1] if which < 5 else tokens[2]
            gathered, token = gather_rows(piece, bits, which % 2 == 0, after)
            full.append(gathered)
            tokens.append(token)
        small_all = full[0][:, width:]
        full[0] = full[0][:, :width]
        all_weights = [tuple(full[5 * layer : 5 * layer + 5]) for layer in range(layers)]
        row_count = layers * 6
        row_params = small_all[:, :row_count].T.astype(jnp.float32).reshape(layers, 6, -1)
        cols = small_all[:, row_count : row_count + lanes_cols].reshape(members, -1)[:, :per_block]
        cols = cols.reshape(members, layers, 6, heads, part).transpose(1, 2, 3, 0, 4)
        cols = cols.reshape(layers, 6, width).astype(jnp.float32)

        state = frames_in.astype(jnp.float32)
        kept = []
        for layer in range(layers):
            state, saved = forward_layer(
                state, all_weights[layer], cols[layer],
                row_params[layer, :2], row_params[layer, 2:], mesh,
            )
            kept.append(saved)
        frames_out = state.astype(jnp.bfloat16)
        grad = cotangent.astype(jnp.float32)
        results = [None] * layers
        cols_parts = [None] * layers
        row_parts = [None] * layers
        for layer in reversed(range(layers)):
            grad, results[layer], cols_parts[layer], row_parts[layer] = backward_layer(
                grad, all_weights[layer], row_params[layer, :2], kept[layer], bits, mesh, None
            )
        row_part = jnp.concatenate(row_parts, axis=0).T
        col_part = jnp.stack(cols_parts).reshape(layers, 6, heads, members, part)
        col_part = col_part.transpose(3, 0, 1, 2, 4).reshape(members, per_block)
        col_part = jnp.pad(col_part, ((0, 0), (0, lanes_cols * block - per_block)))
        small_part = jnp.concatenate([row_part, col_part.reshape(members * block, lanes_cols)], axis=1)
        small_sum = scatter_rows(pad_lanes(small_part), bits, False)
        row_sum = small_sum[:, :row_count].T.reshape(layers, 6, block)
        col_sum = small_sum[:, row_count : row_count + lanes_cols].reshape(-1)[:per_block]
        col_sum = col_sum.reshape(layers, 6, heads, part)

        def stacked(member, shape):
            return jnp.stack([results[layer][member].reshape(shape) for layer in range(layers)])

        return (
            frames_out,
            grad,
            stacked(0, (block, 3, width)),
            stacked(1, (block, width)),
            stacked(2, (block, 4, width)),
            stacked(3, (block, 4, width)),
            col_sum,
            row_sum[:, :2],
            row_sum[:, 2:],
        )

    return shards


def solution(mesh):
    placed = (
        P(("dp", "ctx"), None),
        P(None, ("dp", "ctx"), None, "mp"),
        P(None, ("dp", "ctx"), "mp"),
        P(None, ("dp", "ctx"), None, "mp"),
        P(None, ("dp", "ctx"), None, "mp"),
        P(None, None, "mp", ("dp", "ctx")),
        P(None, None, ("dp", "ctx")),
        P(None, None, ("dp", "ctx")),
        P(("dp", "ctx"), None),
    )
    return jax.shard_map(
        make_shards(mesh),
        mesh=mesh,
        in_specs=placed,
        out_specs=(
            P(("dp", "ctx"), None),
            P(("dp", "ctx"), None),
            P(None, ("dp", "ctx"), None, "mp"),
            P(None, ("dp", "ctx"), "mp"),
            P(None, ("dp", "ctx"), None, "mp"),
            P(None, ("dp", "ctx"), None, "mp"),
            P(None, None, "mp", ("dp", "ctx")),
            P(None, None, ("dp", "ctx")),
            P(None, None, ("dp", "ctx")),
        ),
        check_vma=False,
    )
```
